32 devices in a mesh: shard: 4 (over y, core), ctx: 8 (over z, x).
Axes of the slice: x: 2, y: 2, z: 4, core: 2. Of those that a mesh axis runs over, the one named last changes fastest.
Arguments:
- tokens: bfloat16 [16384, 576], P(('shard', 'ctx')), may hold values from -6 to 6
- cotangent: bfloat16 [16384, 576], P(('shard', 'ctx')), may hold values from -6 to 6
- seq_lengths: int32 [4, 2], P('shard'), may hold values from 1024 to 2048, as said below
- w_query: bfloat16 [2, 576, 576], P(None, 'shard'), may hold values from -0.25 to 0.25
- key_weight: bfloat16 [2, 576, 192], P(None, 'shard'), may hold values from -0.25 to 0.25
- value_weight: bfloat16 [2, 576, 192], P(None, 'shard'), may hold values from -0.25 to 0.25
- w_out: bfloat16 [2, 576, 576], P(None, 'shard'), may hold values from -3 to 3
- w_gate: bfloat16 [2, 576, 1536], P(None, 'shard'), may hold values from -0.25 to 0.25
- w_up: bfloat16 [2, 576, 1536], P(None, 'shard'), may hold values from -0.25 to 0.25
- w_down: bfloat16 [2, 1536, 576], P(None, 'shard'), may hold values from -0.15625 to 0.15625
- attn_gain: bfloat16 [2, 576], P(None, 'shard'), may hold values from 0.5 to 1.5
- ffn_gain: bfloat16 [2, 576], P(None, 'shard'), may hold values from 0.5 to 1.5
Outputs:
- output: bfloat16 [16384, 576], P(('shard', 'ctx'))
- token_grad: bfloat16 [16384, 576], P(('shard', 'ctx'))
- grad_query: float32 [2, 576, 576], P(None, 'shard')
- grad_key: float32 [2, 576, 192], P(None, 'shard')
- grad_value: float32 [2, 576, 192], P(None, 'shard')
- grad_out: float32 [2, 576, 576], P(None, 'shard')
- grad_gate: float32 [2, 576, 1536], P(None, 'shard')
- grad_up: float32 [2, 576, 1536], P(None, 'shard')
- grad_down: float32 [2, 1536, 576], P(None, 'shard')
- grad_attn_gain: float32 [2, 576], P(None, 'shard')
- grad_ffn_gain: float32 [2, 576], P(None, 'shard')
The draws below stay inside these ranges and needn't reach their ends.
Inputs may be any that keep to these rules, and one draw needn't show every extreme that they name: `seq_lengths`: in every group the last sequence has exactly 2048 tokens; the lengths padded to multiples of 128 sum to at most 3968.
All inputs are finite; a program needn't handle non-finite values.
Results may differ from the reference program's by a relative error of at most 0.024.
Values may be sent and summed in bfloat16 or wider, within the bound.
A program may use at most 448 MiB of HBM per device.

```python
import jax
import jax.numpy as jnp
from jax import lax

MODEL_WIDTH = 576
QUERY_HEADS = 9
KEY_VALUE_HEADS = 3
HEAD_SIZE = 64
FF = 1536
DECODER_LAYERS = 2
BLK = 128
LMIN = 1024
SPREAD = 6
GROUPS = 4
LONGEST_TOKENS = 2048
NSEQ = 2
TOKENS = 16384


def draw_seq_lengths(key, part):
    key_blocks, key_tail = jax.random.split(key, 2)
    extra_blocks = jax.random.randint(key_blocks, (GROUPS, NSEQ), 0, SPREAD + 1)
    tail_rows = jax.random.randint(key_tail, (GROUPS, NSEQ), 0, BLK)
    lengths = LMIN + BLK * extra_blocks + tail_rows
    numbers = jnp.arange(NSEQ, dtype=jnp.int32)[None, :]
    lengths = jnp.where(numbers == NSEQ - 1, LONGEST_TOKENS, lengths)
    return lengths.astype(jnp.int32)


def block_levels(key, extent, cuts, least, top_value):
    def one(dim, blocks):
        steps = jax.random.uniform(jax.random.fold_in(jax.random.fold_in(key, 6), dim), (blocks,), jnp.float32, least / len(cuts), top_value / len(cuts))
        return jnp.repeat(jnp.exp(steps), extent[dim] // blocks).reshape((-1,) + (1,) * (len(extent) - dim - 1))

    gain = one(*cuts[0])
    for cut in cuts[1:]:
        gain = gain * one(*cut)
    return gain


def bell_draw(rng, dims, width, bound, shards=(), kind=jnp.bfloat16):
    loudness = block_levels(rng, dims, shards, -0.22, 0.18) if shards else 1.0
    values = jax.random.normal(rng, dims, jnp.float32) * width * loudness
    return jnp.minimum(jnp.maximum(values, -bound), bound).astype(kind)


def setup_inputs(seed: int = 0) -> dict:
    streams_of = jax.random.split(jax.random.key(seed), 13)
    tokens = bell_draw(streams_of[0], (TOKENS, MODEL_WIDTH), 1.0, 6.0, ((0, 32),))
    cotangent = bell_draw(streams_of[1], (TOKENS, MODEL_WIDTH), 1.0, 6.0, ((0, 32),))
    seq_lengths = draw_seq_lengths(jax.random.fold_in(streams_of[12], 71), 0)
    w_query = bell_draw(streams_of[3], (DECODER_LAYERS, MODEL_WIDTH, MODEL_WIDTH), MODEL_WIDTH ** -0.5, 0.25, ((1, 4),))
    key_weight = bell_draw(streams_of[4], (DECODER_LAYERS, MODEL_WIDTH, KEY_VALUE_HEADS * HEAD_SIZE), MODEL_WIDTH ** -0.5, 0.25, ((1, 4),))
    value_weight = bell_draw(streams_of[5], (DECODER_LAYERS, MODEL_WIDTH, KEY_VALUE_HEADS * HEAD_SIZE), MODEL_WIDTH ** -0.5, 0.25, ((1, 4),))
    w_out = bell_draw(streams_of[6], (DECODER_LAYERS, MODEL_WIDTH, MODEL_WIDTH), 4 ** -0.5, 3.0, ((1, 4),))
    w_gate = bell_draw(streams_of[7], (DECODER_LAYERS, MODEL_WIDTH, FF), MODEL_WIDTH ** -0.5, 0.25, ((1, 4),))
    w_up = bell_draw(streams_of[8], (DECODER_LAYERS, MODEL_WIDTH, FF), MODEL_WIDTH ** -0.5, 0.25, ((1, 4),))
    w_down = bell_draw(streams_of[9], (DECODER_LAYERS, FF, MODEL_WIDTH), FF ** -0.5, 0.15625, ((1, 4),))
    attn_gain = jnp.clip(1.0 + 0.1 * jax.random.normal(streams_of[10], (DECODER_LAYERS, MODEL_WIDTH), jnp.float32), 0.5, 1.5).astype(jnp.bfloat16)
    ffn_gain = jnp.clip(1.0 + 0.1 * jax.random.normal(streams_of[11], (DECODER_LAYERS, MODEL_WIDTH), jnp.float32), 0.5, 1.5).astype(jnp.bfloat16)
    return {"tokens": tokens, "cotangent": cotangent, "seq_lengths": seq_lengths, "w_query": w_query, "key_weight": key_weight, "value_weight": value_weight, "w_out": w_out, "w_gate": w_gate, "w_up": w_up, "w_down": w_down, "attn_gain": attn_gain, "ffn_gain": ffn_gain}


EPSILON = 1e-05
ROPE_BASE = 100000.0
HIGHEST = lax.Precision.HIGHEST

@jax.custom_vjp
def low(v):
    return lax.optimization_barrier(v.astype(jnp.bfloat16)).astype(jnp.float32)

@jax.custom_vjp
def low_back(v):
    return v

def low_keep(v):
    return (low(v), None)

def low_pass(kept, grad):
    return (grad,)

def back_keep(v):
    return (v, None)

def back_low(kept, grad):
    return (low(grad),)
low.defvjp(low_keep, low_pass)
low_back.defvjp(back_keep, back_low)

def rms_scale(value_tensor, gain_vec):
    return value_tensor * lax.rsqrt(lax.optimization_barrier(jnp.mean(value_tensor * value_tensor, axis=-1, keepdims=True)) + EPSILON) * gain_vec

def rotary_tables(value_tensor, token_positions):
    half_dim = value_tensor.shape[-1] // 2
    spacing = jnp.arange(half_dim, dtype=jnp.float32) * (2.0 / value_tensor.shape[-1])
    frequency = jnp.float32(ROPE_BASE) ** (-spacing)
    angles = token_positions.astype(jnp.float32)[:, None] * frequency[None, :]
    angles = jnp.concatenate([angles, angles], axis=-1)
    cosine = jnp.cos(angles)[:, None, :]
    sine_part = jnp.sin(angles)[:, None, :]
    turned = jnp.concatenate([-value_tensor[..., half_dim:], value_tensor[..., :half_dim]], axis=-1)
    return value_tensor * cosine + turned * sine_part

def row_info(row_ids, lengths, group_rows):
    padded = ((lengths + BLK - 1) // BLK * BLK).astype(jnp.int32)
    rel_ends = jnp.cumsum(padded).astype(jnp.int32)
    offset = (group_rows - BLK - rel_ends[-1]).astype(jnp.int32)
    seq_ends = (rel_ends + offset).astype(jnp.int32)
    starts = (seq_ends - padded).astype(jnp.int32)
    used_end = seq_ends[-1]
    inside = (row_ids[:, None] >= starts[None, :]) & (row_ids[:, None] < seq_ends[None, :])
    anywhere = jnp.any(inside, axis=1)
    numbers = jnp.arange(lengths.shape[0], dtype=jnp.int32)
    seq_ids = jnp.where(anywhere, lax.optimization_barrier(jnp.sum(jnp.where(inside, numbers[None, :], 0), axis=1)), lengths.shape[0])
    seq_ids = jnp.where(row_ids < 0, -1, seq_ids).astype(jnp.int32)
    outside_first = jnp.where(row_ids < offset, 0, used_end).astype(jnp.int32)
    first_row = jnp.where(anywhere, lax.optimization_barrier(jnp.sum(jnp.where(inside, starts[None, :], 0), axis=1)), outside_first)
    valid = jnp.any(inside & (row_ids[:, None] < (starts + lengths)[None, :]), axis=1)
    return (seq_ids, valid, (row_ids - first_row).astype(jnp.int32))

def attention(queries, key_tensor, value_tensor, key_seq, key_valid, query_seq, head_groups, rows_per_group):
    block_rows = min(512, rows_per_group)
    blocks = rows_per_group // block_rows
    heads_per_group = QUERY_HEADS // KEY_VALUE_HEADS
    score_scale = HEAD_SIZE ** (-0.5)
    key_span = LONGEST_TOKENS + block_rows
    query_grid = queries.reshape(head_groups, rows_per_group, QUERY_HEADS, HEAD_SIZE)
    key_layout = jnp.pad(key_tensor.reshape(head_groups, rows_per_group, KEY_VALUE_HEADS, HEAD_SIZE), ((0, 0), (LONGEST_TOKENS, 0), (0, 0), (0, 0)))
    value_layout = jnp.pad(value_tensor.reshape(head_groups, rows_per_group, KEY_VALUE_HEADS, HEAD_SIZE), ((0, 0), (LONGEST_TOKENS, 0), (0, 0), (0, 0)))

    def one_block(block_id):
        group_id = (block_id // blocks).astype(jnp.int32)
        first_row = (block_id % blocks * block_rows).astype(jnp.int32)
        query_part = lax.dynamic_slice_in_dim(query_grid[group_id], first_row, block_rows, 0)
        key_part = jnp.repeat(lax.dynamic_slice_in_dim(key_layout[group_id], first_row, key_span, 0), heads_per_group, axis=1)
        value_part = jnp.repeat(lax.dynamic_slice_in_dim(value_layout[group_id], first_row, key_span, 0), heads_per_group, axis=1)
        seq_keys = lax.dynamic_slice_in_dim(key_seq[group_id], first_row, key_span, 0)
        valid_keys = lax.dynamic_slice_in_dim(key_valid[group_id], first_row, key_span, 0)
        seq_queries = lax.dynamic_slice_in_dim(query_seq[group_id], first_row, block_rows, 0)
        query_ids = first_row + jnp.arange(block_rows, dtype=jnp.int32)
        key_ids = first_row - LONGEST_TOKENS + jnp.arange(key_span, dtype=jnp.int32)
        allowed = (key_ids[None, :] == query_ids[:, None]) | (key_ids[None, :] <= query_ids[:, None]) & (seq_keys[None, :] == seq_queries[:, None]) & valid_keys[None, :]
        scores = low_back(jnp.einsum('qhd,khd->hqk', query_part, key_part, precision=HIGHEST) * score_scale)
        scores = jnp.where(allowed[None], scores, -jnp.inf)
        peak_scores = lax.optimization_barrier(jnp.max(scores, axis=-1, keepdims=True))
        raised = jnp.exp(scores - peak_scores)
        softmax_w = low(raised / lax.optimization_barrier(jnp.sum(raised, axis=-1, keepdims=True)))
        return jnp.einsum('hqk,khd->qhd', softmax_w, value_part, precision=HIGHEST)
    mixed_rows = lax.map(jax.checkpoint(one_block), jnp.arange(head_groups * blocks, dtype=jnp.int32))
    return mixed_rows.reshape(head_groups * rows_per_group, QUERY_HEADS * HEAD_SIZE)

def reference(tokens, cotangent, seq_lengths, w_query, key_weight, value_weight, w_out, w_gate, w_up, w_down, attn_gain, ffn_gain):
    head_groups = seq_lengths.shape[0]
    rows_per_group = tokens.shape[0] // head_groups
    query_ids = jnp.arange(rows_per_group, dtype=jnp.int32)
    key_ids = jnp.arange(rows_per_group + LONGEST_TOKENS, dtype=jnp.int32) - LONGEST_TOKENS
    query_seq, query_valid, query_pos = jax.vmap(lambda lens: row_info(query_ids, lens, rows_per_group))(seq_lengths)
    key_seq, key_valid, key_pos = jax.vmap(lambda lens: row_info(key_ids, lens, rows_per_group))(seq_lengths)
    token_positions = query_pos.reshape(-1)

    def forward(residual, query_mat, key_mat, value_mat, out_mat, gate_mat, up_mat, down_mat, attn_scale, ffn_scale):
        for layer_no in range(DECODER_LAYERS):
            normed_a = low(rms_scale(residual, attn_scale[layer_no]))
            query_pre = low_back(jnp.dot(normed_a, query_mat[layer_no], precision=HIGHEST))
            key_unrotated = low_back(jnp.dot(normed_a, key_mat[layer_no], precision=HIGHEST))
            value_projected = low_back(jnp.dot(normed_a, value_mat[layer_no], precision=HIGHEST))
            queries = low(rotary_tables(query_pre.reshape(-1, QUERY_HEADS, HEAD_SIZE), token_positions))
            key_tensor = low(rotary_tables(key_unrotated.reshape(-1, KEY_VALUE_HEADS, HEAD_SIZE), token_positions))
            value_tensor = low(value_projected).reshape(-1, KEY_VALUE_HEADS, HEAD_SIZE)
            attended = low_back(low(attention(queries, key_tensor, value_tensor, key_seq, key_valid, query_seq, head_groups, rows_per_group)))
            residual = residual + low_back(jnp.dot(attended, out_mat[layer_no], precision=HIGHEST))
            normed_f = low(rms_scale(residual, ffn_scale[layer_no]))
            gate_act = low_back(jnp.dot(normed_f, gate_mat[layer_no], precision=HIGHEST))
            up_act = low_back(jnp.dot(normed_f, up_mat[layer_no], precision=HIGHEST))
            hidden = low(jax.nn.silu(gate_act) * up_act)
            residual = residual + low_back(jnp.dot(hidden, down_mat[layer_no], precision=HIGHEST))
        return residual
    result, pullback = jax.vjp(forward, tokens.astype(jnp.float32), w_query.astype(jnp.float32), key_weight.astype(jnp.float32), value_weight.astype(jnp.float32), w_out.astype(jnp.float32), w_gate.astype(jnp.float32), w_up.astype(jnp.float32), w_down.astype(jnp.float32), attn_gain.astype(jnp.float32), ffn_gain.astype(jnp.float32))
    gradients = pullback(cotangent.astype(jnp.float32))
    return (result.astype(jnp.bfloat16), gradients[0].astype(jnp.bfloat16), gradients[1], gradients[2], gradients[3], gradients[4], gradients[5], gradients[6], gradients[7], gradients[8], gradients[9])
```

```python
import jax
import jax.numpy as jnp
from jax import lax
from jax.experimental import pallas as pl
from jax.experimental.pallas import tpu as pltpu
from jax.sharding import PartitionSpec as P

QUERY_HEADS = 9
KEY_VALUE_HEADS = 3
HEAD_SIZE = 64
HEADS_PER_GROUP = QUERY_HEADS // KEY_VALUE_HEADS
QUERY_WIDTH = QUERY_HEADS * HEAD_SIZE
KV_WIDTH = KEY_VALUE_HEADS * HEAD_SIZE
GROUP_WIDTH = HEADS_PER_GROUP * HEAD_SIZE
DECODER_LAYERS = 2
BLK = 128
SEQ_MOST = 4096
CHUNK = 512
EPSILON = 1e-05
ROPE_BASE = 100000.0
LOWEST = -1e30
F32 = jnp.float32
BF16 = jnp.bfloat16


def from_behind(value, axis, steps):
    count = lax.axis_size(axis)
    leading, last = (max(0, -steps), min(count, count - steps))
    return lax.ppermute(value, axis, [(source, source + steps) for source in range(leading, last)])


def swap(value, axis, bit):
    count = lax.axis_size(axis)
    return lax.ppermute(value, axis, [(i, i ^ (1 << bit)) for i in range(count)])


def bit_count(axis):
    count = lax.axis_size(axis)
    bits = count.bit_length() - 1
    assert count == 1 << bits
    return bits


def scatter_sum(value, axis):
    index = lax.axis_index(axis)
    for bit in range(bit_count(axis)):
        value = value.reshape((value.shape[0] // 2, 2) + value.shape[1:])
        mine = (index >> bit) & 1
        kept = lax.dynamic_index_in_dim(value, mine, 1, keepdims=False)
        sent = lax.dynamic_index_in_dim(value, 1 - mine, 1, keepdims=False)
        value = (kept.astype(F32) + swap(sent, axis, bit).astype(F32)).astype(BF16)
    return value[0]


def gather_all(value, axis):
    index = lax.axis_index(axis)
    value = value[None]
    for bit in reversed(range(bit_count(axis))):
        other = swap(value, axis, bit)
        low_bit = ((index >> bit) & 1) == 0
        first = jnp.where(low_bit, value, other)
        second = jnp.where(low_bit, other, value)
        value = jnp.stack([first, second], axis=1)
        value = value.reshape((2 * value.shape[0],) + value.shape[2:])
    return value


def reduce_pack(value):
    owned = scatter_sum(value, "shard")
    flat = owned.reshape(-1)
    count = lax.axis_size("ctx")
    unit = count * 16 * 128
    size = flat.shape[0]
    padded = -(-size // unit) * unit
    if padded != size:
        flat = jnp.pad(flat, (0, padded - size))
    part = scatter_sum(flat.reshape(count, -1, 128), "ctx")
    return gather_all(part, "ctx").reshape(-1)[:size].astype(F32)


def rms_scale(value_tensor, gain_vec):
    return (
        value_tensor
        * lax.rsqrt(jnp.mean(value_tensor * value_tensor, axis=-1, keepdims=True) + EPSILON)
        * gain_vec
    )


def rotary_tables(token_positions):
    half_dim = HEAD_SIZE // 2
    spacing = jnp.arange(half_dim, dtype=F32) * (2.0 / HEAD_SIZE)
    frequency = F32(ROPE_BASE) ** (-spacing)
    angles = frequency[:, None] * token_positions.astype(F32)[None, :]
    return jnp.cos(angles), jnp.sin(angles)


def rotate(value, cosine, sine):
    rows = value.shape[1]
    halves = value.reshape(-1, 2, HEAD_SIZE // 2, rows)
    first, second = halves[:, 0], halves[:, 1]
    turned = jnp.stack(
        [first * cosine - second * sine, second * cosine + first * sine], axis=1
    )
    return turned.reshape(value.shape)


def row_limits(row_ids, lengths, group_rows):
    padded = (lengths + BLK - 1) // BLK * BLK
    rel_ends = jnp.cumsum(padded)
    offset = group_rows - BLK - rel_ends[-1]
    seq_ends = rel_ends + offset
    starts = seq_ends - padded
    used_end = seq_ends[-1]
    inside = (row_ids[:, None] >= starts[None, :]) & (row_ids[:, None] < seq_ends[None, :])
    anywhere = jnp.any(inside, axis=1)
    outside_first = jnp.where(row_ids < offset, 0, used_end)
    first_row = jnp.where(
        anywhere, jnp.sum(jnp.where(inside, starts[None, :], 0), axis=1), outside_first
    )
    valid_end = jnp.sum(jnp.where(inside, (starts + lengths)[None, :], 0), axis=1)
    key_from = jnp.where(anywhere, first_row, row_ids)
    key_to = jnp.where(anywhere, jnp.minimum(row_ids + 1, valid_end), row_ids)
    return row_ids - first_row, key_from, key_to


def contract(left, right, left_dim, right_dim):
    return lax.dot_general(
        left, right, (((left_dim,), (right_dim,)), ((), ())), preferred_element_type=F32
    )


def allowed_keys(limits_ref, chunk_start, rows):
    key_ids = lax.broadcasted_iota(jnp.int32, (CHUNK, rows), 0) + chunk_start
    return ((key_ids >= limits_ref[0:1, :]) & (key_ids < limits_ref[1:2, :])) | (
        key_ids == limits_ref[2:3, :]
    )


def attend_kernel(first_ref, query_ref, kv_ref, limits_ref, out_ref, sums_ref, total_ref):
    rows = query_ref.shape[1]
    chunks = kv_ref.shape[2] // CHUNK
    total_ref[...] = jnp.zeros_like(total_ref)

    def step(chunk, carry):
        start = pl.multiple_of(chunk * CHUNK, CHUNK)
        keys = kv_ref[0, :, pl.ds(start, CHUNK)]
        values = kv_ref[1, :, pl.ds(start, CHUNK)]
        allowed = allowed_keys(limits_ref, start, rows)
        carry = list(carry)
        for head in range(HEADS_PER_GROUP):
            cut = slice(head * HEAD_SIZE, (head + 1) * HEAD_SIZE)
            peak, summed = carry[2 * head], carry[2 * head + 1]
            scores = contract(keys, query_ref[cut, :], 0, 0)
            scores = jnp.where(allowed, scores, LOWEST)
            new_peak = jnp.maximum(peak, jnp.max(scores, axis=0, keepdims=True))
            raised = jnp.exp(scores - new_peak)
            fade = jnp.exp(peak - new_peak)
            carry[2 * head] = new_peak
            carry[2 * head + 1] = summed * fade + jnp.sum(raised, axis=0, keepdims=True)
            total_ref[cut, :] = total_ref[cut, :] * fade + contract(
                values, raised.astype(BF16), 1, 0
            )
        return tuple(carry)

    start_carry = (
        jnp.full((1, rows), LOWEST, F32),
        jnp.zeros((1, rows), F32),
    ) * HEADS_PER_GROUP
    carry = lax.fori_loop(first_ref[0], chunks, step, start_carry)
    for head in range(HEADS_PER_GROUP):
        cut = slice(head * HEAD_SIZE, (head + 1) * HEAD_SIZE)
        peak, summed = carry[2 * head], carry[2 * head + 1]
        out_ref[cut, :] = (total_ref[cut, :] / summed).astype(BF16)
        sums_ref[0, head : head + 1, :] = peak + jnp.log(summed)


def attend_back_kernel(
    first_ref,
    query_ref,
    grad_ref,
    kv_ref,
    limits_ref,
    sums_ref,
    delta_ref,
    grad_query_ref,
    grad_kv_ref,
):
    rows = query_ref.shape[1]
    chunks = kv_ref.shape[2] // CHUNK
    first = first_ref[0]
    grad_query_ref[...] = jnp.zeros_like(grad_query_ref)

    def clear(chunk, carry):
        start = pl.multiple_of(chunk * CHUNK, CHUNK)
        grad_kv_ref[:, :, pl.ds(start, CHUNK)] = jnp.zeros((2, HEAD_SIZE, CHUNK), BF16)
        return carry

    lax.fori_loop(0, first, clear, 0)

    def step(chunk, carry):
        start = pl.multiple_of(chunk * CHUNK, CHUNK)
        keys = kv_ref[0, :, pl.ds(start, CHUNK)]
        values = kv_ref[1, :, pl.ds(start, CHUNK)]
        allowed = allowed_keys(limits_ref, start, rows)
        grad_keys = jnp.zeros((HEAD_SIZE, CHUNK), F32)
        grad_values = jnp.zeros((HEAD_SIZE, CHUNK), F32)
        for head in range(HEADS_PER_GROUP):
            cut = slice(head * HEAD_SIZE, (head + 1) * HEAD_SIZE)
            query = query_ref[cut, :]
            grad = grad_ref[cut, :]
            scores = contract(keys, query, 0, 0)
            scores = jnp.where(allowed, scores, LOWEST)
            softmax = jnp.exp(scores - sums_ref[0, head : head + 1, :])
            grad_probs = contract(values, grad, 0, 0)
            grad_scores = softmax * (grad_probs - delta_ref[0, head : head + 1, :])
            low_scores = grad_scores.astype(BF16)
            grad_values += contract(grad, softmax.astype(BF16), 1, 1)
            grad_keys += contract(query, low_scores, 1, 1)
            grad_query_ref[cut, :] += contract(keys, low_scores, 1, 0)
        grad_kv_ref[0, :, pl.ds(start, CHUNK)] = grad_keys.astype(BF16)
        grad_kv_ref[1, :, pl.ds(start, CHUNK)] = grad_values.astype(BF16)
        return carry

    lax.fori_loop(first, chunks, step, 0)


def group_block(rows):
    return pl.BlockSpec((GROUP_WIDTH, rows), lambda group, first: (group, 0))


def window_block(window):
    return pl.BlockSpec((2, HEAD_SIZE, window), lambda group, first: (0, group, 0))


def stat_block(rows):
    return pl.BlockSpec((1, HEADS_PER_GROUP, rows), lambda group, first: (group, 0, 0))


def limits_block(rows):
    return pl.BlockSpec((3, rows), lambda group, first: (0, 0))


def attend(first, queries, window_kv, limits):
    rows, window = queries.shape[1], window_kv.shape[2]
    return pl.pallas_call(
        attend_kernel,
        grid_spec=pltpu.PrefetchScalarGridSpec(
            num_scalar_prefetch=1,
            grid=(KEY_VALUE_HEADS,),
            in_specs=[group_block(rows), window_block(window), limits_block(rows)],
            out_specs=[group_block(rows), stat_block(rows)],
            scratch_shapes=[pltpu.VMEM((GROUP_WIDTH, rows), F32)],
        ),
        out_shape=[
            jax.ShapeDtypeStruct((QUERY_WIDTH, rows), BF16),
            jax.ShapeDtypeStruct((KEY_VALUE_HEADS, HEADS_PER_GROUP, rows), F32),
        ],
        cost_estimate=pl.CostEstimate(
            flops=60 * QUERY_WIDTH * rows * window,
            bytes_accessed=4 * KV_WIDTH * window,
            transcendentals=QUERY_HEADS * rows * window,
        ),
        compiler_params=pltpu.CompilerParams(vmem_limit_bytes=32 << 20),
    )(first, queries, window_kv, limits)


def attend_back(first, queries, grads, window_kv, limits, sums, delta):
    rows, window = queries.shape[1], window_kv.shape[2]
    return pl.pallas_call(
        attend_back_kernel,
        grid_spec=pltpu.PrefetchScalarGridSpec(
            num_scalar_prefetch=1,
            grid=(KEY_VALUE_HEADS,),
            in_specs=[
                group_block(rows),
                group_block(rows),
                window_block(window),
                limits_block(rows),
                stat_block(rows),
                stat_block(rows),
            ],
            out_specs=[group_block(rows), window_block(window)],
        ),
        out_shape=[
            jax.ShapeDtypeStruct((QUERY_WIDTH, rows), F32),
            jax.ShapeDtypeStruct((2, KV_WIDTH, window), BF16),
        ],
        cost_estimate=pl.CostEstimate(
            flops=120 * QUERY_WIDTH * rows * window,
            bytes_accessed=8 * KV_WIDTH * window,
            transcendentals=QUERY_HEADS * rows * window,
        ),
        compiler_params=pltpu.CompilerParams(vmem_limit_bytes=32 << 20),
    )(first, queries, grads, window_kv, limits, sums, delta)


def collect_window(own_pair, reach_back):
    pieces = [from_behind(own_pair, "ctx", distance) for distance in range(reach_back, 0, -1)]
    window = jnp.concatenate(pieces + [own_pair], axis=1)
    return window.reshape(2, KV_WIDTH, -1)


def return_grads(window_grad, reach_back, rows):
    totals = window_grad[:, reach_back * rows :].astype(F32)
    for distance in range(1, reach_back + 1):
        piece = window_grad[:, (reach_back - distance) * rows : (reach_back - distance + 1) * rows]
        totals = totals + from_behind(piece, "ctx", -distance).astype(F32)
    return totals


def layer_forward(residual, weights, tables, first, limits, reach_back):
    qkv_mat, out_mat, gate_up_mat, down_mat, attn_scale, ffn_scale = weights
    cosine, sine = tables
    normed_a = rms_scale(residual, attn_scale).astype(BF16)
    projected = contract(qkv_mat, normed_a, 0, 1)
    rotated = rotate(projected[: QUERY_WIDTH + KV_WIDTH], cosine, sine)
    queries = rotated[:QUERY_WIDTH].astype(BF16) * BF16(HEAD_SIZE ** (-0.5))
    own_pair = jnp.concatenate(
        [rotated[QUERY_WIDTH:].astype(BF16), projected[QUERY_WIDTH + KV_WIDTH :].astype(BF16)],
        axis=0,
    )
    window_kv = collect_window(own_pair, reach_back)
    attended, sums = attend(first, queries, window_kv, limits)
    residual_mid = residual + contract(attended, out_mat, 0, 0)
    normed_f = rms_scale(residual_mid, ffn_scale).astype(BF16)
    gate_up = contract(normed_f, gate_up_mat, 1, 0)
    half = gate_up.shape[1] // 2
    gate_act, up_act = gate_up[:, :half], gate_up[:, half:]
    hidden = (jax.nn.silu(gate_act) * up_act).astype(BF16)
    residual_out = residual_mid + contract(hidden, down_mat, 1, 0)
    record = (
        residual,
        normed_a,
        queries,
        window_kv,
        attended,
        sums,
        residual_mid,
        normed_f,
        gate_act,
        up_act,
        hidden,
    )
    return residual_out, record


def layer_backward(grad_res, weights, record, tables, first, limits, reach_back):
    qkv_mat, out_mat, gate_up_mat, down_mat, attn_scale, ffn_scale = weights
    cosine, sine = tables
    (
        residual,
        normed_a,
        queries,
        window_kv,
        attended,
        sums,
        residual_mid,
        normed_f,
        gate_act,
        up_act,
        hidden,
    ) = record
    rows = residual.shape[0]
    shards = lax.axis_size("shard")
    branch_f = grad_res.astype(BF16)
    grad_down_mat = contract(hidden, branch_f, 0, 0).astype(BF16)
    grad_hidden = contract(branch_f, down_mat, 1, 1)
    sigmoid_g = jax.nn.sigmoid(gate_act)
    grad_gate_up = jnp.concatenate(
        [
            (grad_hidden * up_act * sigmoid_g * (1.0 + gate_act * (1.0 - sigmoid_g))).astype(BF16),
            (grad_hidden * gate_act * sigmoid_g).astype(BF16),
        ],
        axis=1,
    )
    grad_gate_up_mat = contract(normed_f, grad_gate_up, 0, 0).astype(BF16)
    reduced_gate_up = reduce_pack(grad_gate_up_mat.reshape(shards, -1, grad_gate_up.shape[1]))
    grad_normed_f = contract(grad_gate_up, gate_up_mat, 1, 1)
    _, norm_back = jax.vjp(rms_scale, residual_mid, ffn_scale)
    grad_mid_part, grad_ffn_scale = norm_back(grad_normed_f)
    grad_mid = grad_res + grad_mid_part
    branch_a = grad_mid.astype(BF16)
    grad_out_mat = contract(attended, branch_a, 1, 0).astype(BF16)
    width = branch_a.shape[1]
    reduced_down_out = reduce_pack(
        jnp.concatenate(
            [grad_down_mat.reshape(shards, -1, width), grad_out_mat.reshape(shards, -1, width)],
            axis=1,
        )
    )
    grad_attended = contract(out_mat, branch_a, 1, 1).astype(BF16)
    delta = jnp.sum(
        (grad_attended.astype(F32) * attended.astype(F32)).reshape(
            KEY_VALUE_HEADS, HEADS_PER_GROUP, HEAD_SIZE, rows
        ),
        axis=2,
    )
    grad_queries, window_grad = attend_back(
        first, queries, grad_attended, window_kv, limits, sums, delta
    )
    local_grad = return_grads(window_grad.reshape(2 * KV_WIDTH, -1), reach_back, rows)
    grad_queries = rotate(grad_queries * HEAD_SIZE ** (-0.5), cosine, -sine).astype(BF16)
    grad_keys = rotate(local_grad[:KV_WIDTH], cosine, -sine).astype(BF16)
    grad_qkv = jnp.concatenate(
        [grad_queries, grad_keys, local_grad[KV_WIDTH:].astype(BF16)], axis=0
    )
    grad_qkv_mat = contract(normed_a, grad_qkv, 0, 1).astype(BF16)
    grad_normed_a = contract(grad_qkv, qkv_mat, 0, 1)
    _, norm_back = jax.vjp(rms_scale, residual, attn_scale)
    grad_in_part, grad_attn_scale = norm_back(grad_normed_a)
    flat = jnp.concatenate(
        [
            grad_qkv_mat.reshape(shards, -1),
            grad_attn_scale.astype(BF16).reshape(shards, -1),
            grad_ffn_scale.astype(BF16).reshape(shards, -1),
        ],
        axis=1,
    )
    reduced_qkv = reduce_pack(flat)
    owned = width // shards
    hidden_width = hidden.shape[1]
    down_size = hidden_width // shards * width
    gate_up = reduced_gate_up.reshape(owned, 2 * hidden_width)
    qkv_size = owned * (QUERY_WIDTH + 2 * KV_WIDTH)
    qkv = reduced_qkv[:qkv_size].reshape(owned, -1)
    gradients = (
        qkv[:, :QUERY_WIDTH],
        qkv[:, QUERY_WIDTH : QUERY_WIDTH + KV_WIDTH],
        qkv[:, QUERY_WIDTH + KV_WIDTH :],
        reduced_down_out[down_size:].reshape(owned, width),
        gate_up[:, :hidden_width],
        gate_up[:, hidden_width:],
        reduced_down_out[:down_size].reshape(-1, width),
        reduced_qkv[qkv_size : qkv_size + owned],
        reduced_qkv[qkv_size + owned :],
    )
    return grad_mid + grad_in_part, gradients


def body(
    tokens,
    cotangent,
    seq_lengths,
    w_query,
    key_weight,
    value_weight,
    w_out,
    w_gate,
    w_up,
    w_down,
    attn_gain,
    ffn_gain,
):
    rows = tokens.shape[0]
    group_rows = rows * lax.axis_size("ctx")
    longest = min(SEQ_MOST, group_rows // 2)
    reach_back = (longest - 1) // rows + 1
    base = (lax.axis_index("ctx") - reach_back) * rows
    own_ids = lax.axis_index("ctx") * rows + jnp.arange(rows, dtype=jnp.int32)
    token_positions, key_from, key_to = row_limits(own_ids, seq_lengths[0], group_rows)
    limits = jnp.stack([key_from, key_to, own_ids], axis=0) - base
    first = jnp.clip(jnp.min(limits[0]) // CHUNK, 0, reach_back * rows // CHUNK)[None]
    tables = rotary_tables(token_positions)

    gains = gather_all(jnp.concatenate([attn_gain, ffn_gain], axis=0), "shard")
    gains = jnp.transpose(gains, (1, 0, 2)).reshape(2 * DECODER_LAYERS, -1).astype(F32)
    layer_weights = []
    for layer_no in range(DECODER_LAYERS):
        qkv_mat = gather_all(
            jnp.concatenate(
                [w_query[layer_no], key_weight[layer_no], value_weight[layer_no]], axis=1
            ),
            "shard",
        )
        out_mat = gather_all(w_out[layer_no], "shard")
        gate_up_mat = gather_all(
            jnp.concatenate([w_gate[layer_no], w_up[layer_no]], axis=1), "shard"
        )
        down_mat = gather_all(w_down[layer_no], "shard")
        layer_weights.append(
            tuple(
                matrix.reshape(-1, matrix.shape[-1])
                for matrix in (qkv_mat, out_mat, gate_up_mat, down_mat)
            )
            + (gains[layer_no], gains[DECODER_LAYERS + layer_no])
        )

    residual = tokens.astype(F32)
    records = []
    for layer_no in range(DECODER_LAYERS):
        residual, record = layer_forward(
            residual, layer_weights[layer_no], tables, first, limits, reach_back
        )
        records.append(record)
    output = residual.astype(BF16)
    grad_res = cotangent.astype(F32)
    reduced_layers = [None] * DECODER_LAYERS
    for layer_no in range(DECODER_LAYERS - 1, -1, -1):
        grad_res, reduced_layers[layer_no] = layer_backward(
            grad_res,
            layer_weights[layer_no],
            records[layer_no],
            tables,
            first,
            limits,
            reach_back,
        )
    token_grad = grad_res.astype(BF16)
    stacked = tuple(
        jnp.stack([reduced_layers[layer_no][member] for layer_no in range(DECODER_LAYERS)], axis=0)
        for member in range(9)
    )
    return (output, token_grad) + stacked


def solution(mesh):
    placed = (
        P(("shard", "ctx"), None),
        P(("shard", "ctx"), None),
        P("shard", None),
        P(None, "shard", None),
        P(None, "shard", None),
        P(None, "shard", None),
        P(None, "shard", None),
        P(None, "shard", None),
        P(None, "shard", None),
        P(None, "shard", None),
        P(None, "shard"),
        P(None, "shard"),
    )
    return jax.shard_map(
        body,
        mesh=mesh,
        in_specs=placed,
        out_specs=(
            P(("shard", "ctx"), None),
            P(("shard", "ctx"), None),
            P(None, "shard", None),
            P(None, "shard", None),
            P(None, "shard", None),
            P(None, "shard", None),
            P(None, "shard", None),
            P(None, "shard", None),
            P(None, "shard", None),
            P(None, "shard"),
            P(None, "shard"),
        ),
        check_vma=False,
    )
```

```python
import jax
import jax.numpy as jnp
from jax import lax
from jax.experimental import pallas as pl
from jax.experimental.pallas import tpu as pltpu
from jax.sharding import PartitionSpec as P

QUERY_HEADS = 9
KEY_VALUE_HEADS = 3
HEAD_SIZE = 64
HEADS_PER_GROUP = QUERY_HEADS // KEY_VALUE_HEADS
QUERY_WIDTH = QUERY_HEADS * HEAD_SIZE
KV_WIDTH = KEY_VALUE_HEADS * HEAD_SIZE
GROUP_WIDTH = HEADS_PER_GROUP * HEAD_SIZE
DECODER_LAYERS = 2
BLK = 128
SEQ_MOST = 4096
CHUNK = 512
EPSILON = 1e-05
ROPE_BASE = 100000.0
LOWEST = -1e30
F32 = jnp.float32
BF16 = jnp.bfloat16


def from_behind(value, axis, steps):
    count = lax.axis_size(axis)
    leading, last = (max(0, -steps), min(count, count - steps))
    return lax.ppermute(value, axis, [(source, source + steps) for source in range(leading, last)])


def swap(value, axis, bit):
    count = lax.axis_size(axis)
    return lax.ppermute(value, axis, [(i, i ^ (1 << bit)) for i in range(count)])


def bit_count(axis):
    count = lax.axis_size(axis)
    bits = count.bit_length() - 1
    assert count == 1 << bits
    return bits


def scatter_sum(value, axis):
    index = lax.axis_index(axis)
    for bit in range(bit_count(axis)):
        value = value.reshape((value.shape[0] // 2, 2) + value.shape[1:])
        mine = (index >> bit) & 1
        kept = lax.dynamic_index_in_dim(value, mine, 1, keepdims=False)
        sent = lax.dynamic_index_in_dim(value, 1 - mine, 1, keepdims=False)
        value = (kept.astype(F32) + swap(sent, axis, bit).astype(F32)).astype(BF16)
    return value[0]


def gather_all(value, axis):
    index = lax.axis_index(axis)
    value = value[None]
    for bit in reversed(range(bit_count(axis))):
        other = swap(value, axis, bit)
        low_bit = ((index >> bit) & 1) == 0
        first = jnp.where(low_bit, value, other)
        second = jnp.where(low_bit, other, value)
        value = jnp.stack([first, second], axis=1)
        value = value.reshape((2 * value.shape[0],) + value.shape[2:])
    return value


def after(values, event):
    return lax.optimization_barrier((values, event))[0]


def gather_rows(value, axis):
    index = lax.axis_index(axis)
    count = lax.axis_size(axis)
    rows = value.shape[0]
    pieces = [(0, value)]
    for bit in reversed(range(bit_count(axis))):
        pieces += [(away | (1 << bit), swap(piece, axis, bit)) for away, piece in pieces]
    whole = jnp.zeros((count * rows, value.shape[1]), value.dtype)
    for away, piece in pieces:
        whole = lax.dynamic_update_slice(whole, piece, ((index ^ away) * rows, 0))
    return whole


def reduce_ctx(owned):
    flat = jnp.concatenate([part.reshape(-1) for part in owned])
    count = lax.axis_size("ctx")
    unit = count * 16 * 128
    size = flat.shape[0]
    padded = -(-size // unit) * unit
    if padded != size:
        flat = jnp.pad(flat, (0, padded - size))
    part = scatter_sum(flat.reshape(count, -1, 128), "ctx")
    return gather_all(part, "ctx").reshape(-1)[:size].astype(F32)


def rms_scale(value_tensor, gain_vec):
    return (
        value_tensor
        * lax.rsqrt(jnp.mean(value_tensor * value_tensor, axis=-1, keepdims=True) + EPSILON)
        * gain_vec
    )


def rotary_tables(token_positions):
    half_dim = HEAD_SIZE // 2
    spacing = jnp.arange(half_dim, dtype=F32) * (2.0 / HEAD_SIZE)
    frequency = F32(ROPE_BASE) ** (-spacing)
    angles = frequency[:, None] * token_positions.astype(F32)[None, :]
    return jnp.cos(angles), jnp.sin(angles)


def rotate(value, cosine, sine):
    rows = value.shape[1]
    halves = value.reshape(-1, 2, HEAD_SIZE // 2, rows)
    first, second = halves[:, 0], halves[:, 1]
    turned = jnp.stack(
        [first * cosine - second * sine, second * cosine + first * sine], axis=1
    )
    return turned.reshape(value.shape)


def row_limits(row_ids, lengths, group_rows):
    padded = (lengths + BLK - 1) // BLK * BLK
    rel_ends = jnp.cumsum(padded)
    offset = group_rows - BLK - rel_ends[-1]
    seq_ends = rel_ends + offset
    starts = seq_ends - padded
    used_end = seq_ends[-1]
    inside = (row_ids[:, None] >= starts[None, :]) & (row_ids[:, None] < seq_ends[None, :])
    anywhere = jnp.any(inside, axis=1)
    outside_first = jnp.where(row_ids < offset, 0, used_end)
    first_row = jnp.where(
        anywhere, jnp.sum(jnp.where(inside, starts[None, :], 0), axis=1), outside_first
    )
    valid_end = jnp.sum(jnp.where(inside, (starts + lengths)[None, :], 0), axis=1)
    key_from = jnp.where(anywhere, first_row, row_ids)
    key_to = jnp.where(anywhere, jnp.minimum(row_ids + 1, valid_end), row_ids)
    return row_ids - first_row, key_from, key_to


def contract(left, right, left_dim, right_dim):
    return lax.dot_general(
        left, right, (((left_dim,), (right_dim,)), ((), ())), preferred_element_type=F32
    )


def allowed_keys(limits_ref, chunk_start, rows):
    key_ids = lax.broadcasted_iota(jnp.int32, (CHUNK, rows), 0) + chunk_start
    return ((key_ids >= limits_ref[0:1, :]) & (key_ids < limits_ref[1:2, :])) | (
        key_ids == limits_ref[2:3, :]
    )


def attend_kernel(first_ref, query_ref, kv_ref, limits_ref, out_ref, sums_ref, total_ref):
    rows = query_ref.shape[1]
    chunks = kv_ref.shape[2] // CHUNK
    total_ref[...] = jnp.zeros_like(total_ref)

    def step(chunk, carry):
        start = pl.multiple_of(chunk * CHUNK, CHUNK)
        keys = kv_ref[0, :, pl.ds(start, CHUNK)]
        values = kv_ref[1, :, pl.ds(start, CHUNK)]
        allowed = allowed_keys(limits_ref, start, rows)
        carry = list(carry)
        for head in range(HEADS_PER_GROUP):
            cut = slice(head * HEAD_SIZE, (head + 1) * HEAD_SIZE)
            peak, summed = carry[2 * head], carry[2 * head + 1]
            scores = contract(keys, query_ref[cut, :], 0, 0)
            scores = jnp.where(allowed, scores, LOWEST)
            new_peak = jnp.maximum(peak, jnp.max(scores, axis=0, keepdims=True))
            raised = jnp.exp(scores - new_peak)
            fade = jnp.exp(peak - new_peak)
            carry[2 * head] = new_peak
            carry[2 * head + 1] = summed * fade + jnp.sum(raised, axis=0, keepdims=True)
            total_ref[cut, :] = total_ref[cut, :] * fade + contract(
                values, raised.astype(BF16), 1, 0
            )
        return tuple(carry)

    start_carry = (
        jnp.full((1, rows), LOWEST, F32),
        jnp.zeros((1, rows), F32),
    ) * HEADS_PER_GROUP
    carry = lax.fori_loop(first_ref[0], chunks, step, start_carry)
    for head in range(HEADS_PER_GROUP):
        cut = slice(head * HEAD_SIZE, (head + 1) * HEAD_SIZE)
        peak, summed = carry[2 * head], carry[2 * head + 1]
        out_ref[cut, :] = (total_ref[cut, :] / summed).astype(BF16)
        sums_ref[0, head : head + 1, :] = peak + jnp.log(summed)


def attend_back_kernel(
    first_ref,
    query_ref,
    grad_ref,
    kv_ref,
    limits_ref,
    sums_ref,
    delta_ref,
    grad_query_ref,
    grad_kv_ref,
):
    rows = query_ref.shape[1]
    chunks = kv_ref.shape[2] // CHUNK
    first = first_ref[0]
    grad_query_ref[...] = jnp.zeros_like(grad_query_ref)

    def clear(chunk, carry):
        start = pl.multiple_of(chunk * CHUNK, CHUNK)
        grad_kv_ref[:, :, pl.ds(start, CHUNK)] = jnp.zeros((2, HEAD_SIZE, CHUNK), BF16)
        return carry

    lax.fori_loop(0, first, clear, 0)

    def step(chunk, carry):
        start = pl.multiple_of(chunk * CHUNK, CHUNK)
        keys = kv_ref[0, :, pl.ds(start, CHUNK)]
        values = kv_ref[1, :, pl.ds(start, CHUNK)]
        allowed = allowed_keys(limits_ref, start, rows)
        grad_keys = jnp.zeros((HEAD_SIZE, CHUNK), F32)
        grad_values = jnp.zeros((HEAD_SIZE, CHUNK), F32)
        for head in range(HEADS_PER_GROUP):
            cut = slice(head * HEAD_SIZE, (head + 1) * HEAD_SIZE)
            query = query_ref[cut, :]
            grad = grad_ref[cut, :]
            scores = contract(keys, query, 0, 0)
            scores = jnp.where(allowed, scores, LOWEST)
            softmax = jnp.exp(scores - sums_ref[0, head : head + 1, :])
            grad_probs = contract(values, grad, 0, 0)
            grad_scores = softmax * (grad_probs - delta_ref[0, head : head + 1, :])
            low_scores = grad_scores.astype(BF16)
            grad_values += contract(grad, softmax.astype(BF16), 1, 1)
            grad_keys += contract(query, low_scores, 1, 1)
            grad_query_ref[cut, :] += contract(keys, low_scores, 1, 0)
        grad_kv_ref[0, :, pl.ds(start, CHUNK)] = grad_keys.astype(BF16)
        grad_kv_ref[1, :, pl.ds(start, CHUNK)] = grad_values.astype(BF16)
        return carry

    lax.fori_loop(first, chunks, step, 0)


def group_block(rows):
    return pl.BlockSpec((GROUP_WIDTH, rows), lambda group, first: (group, 0))


def window_block(window):
    return pl.BlockSpec((2, HEAD_SIZE, window), lambda group, first: (0, group, 0))


def stat_block(rows):
    return pl.BlockSpec((1, HEADS_PER_GROUP, rows), lambda group, first: (group, 0, 0))


def limits_block(rows):
    return pl.BlockSpec((3, rows), lambda group, first: (0, 0))


def attend(first, queries, window_kv, limits):
    rows, window = queries.shape[1], window_kv.shape[2]
    return pl.pallas_call(
        attend_kernel,
        grid_spec=pltpu.PrefetchScalarGridSpec(
            num_scalar_prefetch=1,
            grid=(KEY_VALUE_HEADS,),
            in_specs=[group_block(rows), window_block(window), limits_block(rows)],
            out_specs=[group_block(rows), stat_block(rows)],
            scratch_shapes=[pltpu.VMEM((GROUP_WIDTH, rows), F32)],
        ),
        out_shape=[
            jax.ShapeDtypeStruct((QUERY_WIDTH, rows), BF16),
            jax.ShapeDtypeStruct((KEY_VALUE_HEADS, HEADS_PER_GROUP, rows), F32),
        ],
        cost_estimate=pl.CostEstimate(
            flops=60 * QUERY_WIDTH * rows * window,
            bytes_accessed=4 * KV_WIDTH * window,
            transcendentals=QUERY_HEADS * rows * window,
        ),
        compiler_params=pltpu.CompilerParams(vmem_limit_bytes=32 << 20),
    )(first, queries, window_kv, limits)


def attend_back(first, queries, grads, window_kv, limits, sums, delta):
    rows, window = queries.shape[1], window_kv.shape[2]
    return pl.pallas_call(
        attend_back_kernel,
        grid_spec=pltpu.PrefetchScalarGridSpec(
            num_scalar_prefetch=1,
            grid=(KEY_VALUE_HEADS,),
            in_specs=[
                group_block(rows),
                group_block(rows),
                window_block(window),
                limits_block(rows),
                stat_block(rows),
                stat_block(rows),
            ],
            out_specs=[group_block(rows), window_block(window)],
        ),
        out_shape=[
            jax.ShapeDtypeStruct((QUERY_WIDTH, rows), F32),
            jax.ShapeDtypeStruct((2, KV_WIDTH, window), BF16),
        ],
        cost_estimate=pl.CostEstimate(
            flops=120 * QUERY_WIDTH * rows * window,
            bytes_accessed=8 * KV_WIDTH * window,
            transcendentals=QUERY_HEADS * rows * window,
        ),
        compiler_params=pltpu.CompilerParams(vmem_limit_bytes=32 << 20),
    )(first, queries, grads, window_kv, limits, sums, delta)


def collect_window(own_pair, reach_back):
    pieces = [from_behind(own_pair, "ctx", distance) for distance in range(reach_back, 0, -1)]
    window = jnp.concatenate(pieces + [own_pair], axis=1)
    return window.reshape(2, KV_WIDTH, -1)


def return_grads(window_grad, reach_back, rows):
    totals = window_grad[:, reach_back * rows :].astype(F32)
    for distance in range(1, reach_back + 1):
        piece = window_grad[:, (reach_back - distance) * rows : (reach_back - distance + 1) * rows]
        totals = totals + from_behind(piece, "ctx", -distance).astype(F32)
    return totals


def layer_forward(residual, weights, tables, first, limits, reach_back):
    qkv_mat, out_mat, gate_up_mat, down_mat, attn_scale, ffn_scale = weights
    cosine, sine = tables
    normed_a = rms_scale(residual, attn_scale).astype(BF16)
    projected = contract(qkv_mat, normed_a, 0, 1)
    rotated = rotate(projected[: QUERY_WIDTH + KV_WIDTH], cosine, sine)
    queries = rotated[:QUERY_WIDTH].astype(BF16) * BF16(HEAD_SIZE ** (-0.5))
    own_pair = jnp.concatenate(
        [rotated[QUERY_WIDTH:].astype(BF16), projected[QUERY_WIDTH + KV_WIDTH :].astype(BF16)],
        axis=0,
    )
    window_kv = collect_window(own_pair, reach_back)
    attended, sums = attend(first, queries, window_kv, limits)
    residual_mid = residual + contract(attended, out_mat, 0, 0)
    normed_f = rms_scale(residual_mid, ffn_scale).astype(BF16)
    gate_up = contract(normed_f, gate_up_mat, 1, 0)
    half = gate_up.shape[1] // 2
    gate_act, up_act = gate_up[:, :half], gate_up[:, half:]
    hidden = (jax.nn.silu(gate_act) * up_act).astype(BF16)
    residual_out = residual_mid + contract(hidden, down_mat, 1, 0)
    record = (
        residual,
        normed_a,
        queries,
        window_kv,
        attended,
        sums,
        residual_mid,
        normed_f,
        gate_act,
        up_act,
        hidden,
    )
    return residual_out, record


def layer_backward(grad_res, weights, record, tables, first, limits, reach_back, later_owned):
    qkv_mat, out_mat, gate_up_mat, down_mat, attn_scale, ffn_scale = weights
    cosine, sine = tables
    (
        residual,
        normed_a,
        queries,
        window_kv,
        attended,
        sums,
        residual_mid,
        normed_f,
        gate_act,
        up_act,
        hidden,
    ) = record
    rows = residual.shape[0]
    shards = lax.axis_size("shard")
    branch_f = grad_res.astype(BF16)
    grad_down_mat = contract(hidden, branch_f, 0, 0).astype(BF16)
    grad_hidden = contract(branch_f, down_mat, 1, 1)
    sigmoid_g = jax.nn.sigmoid(gate_act)
    grad_gate_up = jnp.concatenate(
        [
            (grad_hidden * up_act * sigmoid_g * (1.0 + gate_act * (1.0 - sigmoid_g))).astype(BF16),
            (grad_hidden * gate_act * sigmoid_g).astype(BF16),
        ],
        axis=1,
    )
    grad_gate_up_mat = contract(normed_f, grad_gate_up, 0, 0).astype(BF16)
    owned_gate_up = scatter_sum(
        grad_gate_up_mat.reshape(shards, -1, grad_gate_up.shape[1]), "shard"
    )
    grad_normed_f = contract(grad_gate_up, gate_up_mat, 1, 1)
    _, norm_back = jax.vjp(rms_scale, residual_mid, ffn_scale)
    grad_mid_part, grad_ffn_scale = norm_back(grad_normed_f)
    grad_mid = grad_res + grad_mid_part
    branch_a = grad_mid.astype(BF16)
    grad_out_mat = contract(attended, branch_a, 1, 0).astype(BF16)
    width = branch_a.shape[1]
    owned_down = scatter_sum(grad_down_mat.reshape(shards, -1, width), "shard")
    owned_out = scatter_sum(grad_out_mat.reshape(shards, -1, width), "shard")
    grad_attended = contract(out_mat, branch_a, 1, 1).astype(BF16)
    later_reduced = [reduce_ctx(pack) for pack in later_owned]
    if later_owned:
        grad_attended = after(grad_attended, later_owned)
    delta = jnp.sum(
        (grad_attended.astype(F32) * attended.astype(F32)).reshape(
            KEY_VALUE_HEADS, HEADS_PER_GROUP, HEAD_SIZE, rows
        ),
        axis=2,
    )
    grad_queries, window_grad = attend_back(
        first, queries, grad_attended, window_kv, limits, sums, delta
    )
    local_grad = return_grads(window_grad.reshape(2 * KV_WIDTH, -1), reach_back, rows)
    owned_gate_up, owned_down, owned_out, local_grad = lax.optimization_barrier(
        (owned_gate_up, owned_down, owned_out, local_grad)
    )
    if later_reduced:
        local_grad = after(local_grad, later_reduced)
    grad_queries = rotate(grad_queries * HEAD_SIZE ** (-0.5), cosine, -sine).astype(BF16)
    grad_keys = rotate(local_grad[:KV_WIDTH], cosine, -sine).astype(BF16)
    grad_qkv = jnp.concatenate(
        [grad_queries, grad_keys, local_grad[KV_WIDTH:].astype(BF16)], axis=0
    )
    grad_qkv_mat = contract(normed_a, grad_qkv, 0, 1).astype(BF16)
    grad_normed_a = contract(grad_qkv, qkv_mat, 0, 1)
    _, norm_back = jax.vjp(rms_scale, residual, attn_scale)
    grad_in_part, grad_attn_scale = norm_back(grad_normed_a)
    owned_qkv = scatter_sum(grad_qkv_mat.reshape(shards, -1, grad_qkv.shape[0]), "shard")
    scales = jnp.concatenate(
        [
            grad_attn_scale.astype(BF16).reshape(shards, -1),
            grad_ffn_scale.astype(BF16).reshape(shards, -1),
        ],
        axis=1,
    )
    owned = [
        [owned_gate_up],
        [owned_down, owned_out],
        [owned_qkv, scatter_sum(scales, "shard")],
    ]
    return grad_mid + grad_in_part, owned, later_reduced


def split_gradients(reduced, shards, width, hidden_width):
    reduced_gate_up, reduced_down_out, reduced_qkv = reduced
    owned = width // shards
    down_size = hidden_width // shards * width
    gate_up = reduced_gate_up.reshape(owned, 2 * hidden_width)
    qkv_size = owned * (QUERY_WIDTH + 2 * KV_WIDTH)
    qkv = reduced_qkv[:qkv_size].reshape(owned, -1)
    return (
        qkv[:, :QUERY_WIDTH],
        qkv[:, QUERY_WIDTH : QUERY_WIDTH + KV_WIDTH],
        qkv[:, QUERY_WIDTH + KV_WIDTH :],
        reduced_down_out[down_size:].reshape(owned, width),
        gate_up[:, :hidden_width],
        gate_up[:, hidden_width:],
        reduced_down_out[:down_size].reshape(-1, width),
        reduced_qkv[qkv_size : qkv_size + owned],
        reduced_qkv[qkv_size + owned :],
    )


def body(
    tokens,
    cotangent,
    seq_lengths,
    w_query,
    key_weight,
    value_weight,
    w_out,
    w_gate,
    w_up,
    w_down,
    attn_gain,
    ffn_gain,
):
    rows = tokens.shape[0]
    group_rows = rows * lax.axis_size("ctx")
    longest = min(SEQ_MOST, group_rows // 2)
    reach_back = (longest - 1) // rows + 1
    base = (lax.axis_index("ctx") - reach_back) * rows
    own_ids = lax.axis_index("ctx") * rows + jnp.arange(rows, dtype=jnp.int32)
    token_positions, key_from, key_to = row_limits(own_ids, seq_lengths[0], group_rows)
    limits = jnp.stack([key_from, key_to, own_ids], axis=0) - base
    first = jnp.clip(jnp.min(limits[0]) // CHUNK, 0, reach_back * rows // CHUNK)[None]
    tables = rotary_tables(token_positions)

    gains = gather_all(jnp.concatenate([attn_gain, ffn_gain], axis=0), "shard")
    gains = jnp.transpose(gains, (1, 0, 2)).reshape(2 * DECODER_LAYERS, -1).astype(F32)
    layer_weights = []
    event = gains
    for layer_no in range(DECODER_LAYERS):
        own_qkv = jnp.concatenate(
            [w_query[layer_no], key_weight[layer_no], value_weight[layer_no]], axis=1
        )
        if layer_no:
            own_qkv = after(own_qkv, event)
        qkv_mat = gather_rows(own_qkv, "shard")
        own_out, own_gate, own_up, own_down = after(
            (w_out[layer_no], w_gate[layer_no], w_up[layer_no], w_down[layer_no]), qkv_mat
        )
        out_mat = gather_rows(own_out, "shard")
        gate_up_mat = gather_rows(jnp.concatenate([own_gate, own_up], axis=1), "shard")
        down_mat = gather_rows(own_down, "shard")
        event = (gate_up_mat, down_mat)
        layer_weights.append(
            (qkv_mat, out_mat, gate_up_mat, down_mat)
            + (gains[layer_no], gains[DECODER_LAYERS + layer_no])
        )

    residual = tokens.astype(F32)
    records = []
    for layer_no in range(DECODER_LAYERS):
        residual, record = layer_forward(
            residual, layer_weights[layer_no], tables, first, limits, reach_back
        )
        records.append(record)
    output = residual.astype(BF16)
    grad_res = cotangent.astype(F32)
    reduced_layers = [None] * DECODER_LAYERS
    owned = []
    for layer_no in range(DECODER_LAYERS - 1, -1, -1):
        grad_res, owned, later_reduced = layer_backward(
            grad_res,
            layer_weights[layer_no],
            records[layer_no],
            tables,
            first,
            limits,
            reach_back,
            owned,
        )
        if layer_no < DECODER_LAYERS - 1:
            reduced_layers[layer_no + 1] = later_reduced
    reduced_layers[0] = [reduce_ctx(pack) for pack in owned]
    shards, width, hidden_width = lax.axis_size("shard"), tokens.shape[1], w_gate.shape[2]
    reduced_layers = [
        split_gradients(reduced, shards, width, hidden_width) for reduced in reduced_layers
    ]
    token_grad = grad_res.astype(BF16)
    stacked = tuple(
        jnp.stack([reduced_layers[layer_no][member] for layer_no in range(DECODER_LAYERS)], axis=0)
        for member in range(9)
    )
    return (output, token_grad) + stacked


def solution(mesh):
    placed = (
        P(("shard", "ctx"), None),
        P(("shard", "ctx"), None),
        P("shard", None),
        P(None, "shard", None),
        P(None, "shard", None),
        P(None, "shard", None),
        P(None, "shard", None),
        P(None, "shard", None),
        P(None, "shard", None),
        P(None, "shard", None),
        P(None, "shard"),
        P(None, "shard"),
    )
    return jax.shard_map(
        body,
        mesh=mesh,
        in_specs=placed,
        out_specs=(
            P(("shard", "ctx"), None),
            P(("shard", "ctx"), None),
            P(None, "shard", None),
            P(None, "shard", None),
            P(None, "shard", None),
            P(None, "shard", None),
            P(None, "shard", None),
            P(None, "shard", None),
            P(None, "shard", None),
            P(None, "shard"),
            P(None, "shard"),
        ),
        check_vma=False,
    )
```

```python
import jax
import jax.numpy as jnp
from jax import lax
from jax.experimental import pallas as pl
from jax.experimental.pallas import tpu as pltpu
from jax.sharding import PartitionSpec as P

QUERY_HEADS = 9
KEY_VALUE_HEADS = 3
HEAD_SIZE = 64
HEADS_PER_GROUP = QUERY_HEADS // KEY_VALUE_HEADS
QUERY_WIDTH = QUERY_HEADS * HEAD_SIZE
KV_WIDTH = KEY_VALUE_HEADS * HEAD_SIZE
GROUP_WIDTH = HEADS_PER_GROUP * HEAD_SIZE
DECODER_LAYERS = 2
BLK = 128
SEQ_MOST = 4096
CHUNK = 512
EPSILON = 1e-05
ROPE_BASE = 100000.0
LOWEST = -1e30
F32 = jnp.float32
BF16 = jnp.bfloat16


def from_behind(value, axis, steps):
    count = lax.axis_size(axis)
    leading, last = (max(0, -steps), min(count, count - steps))
    return lax.ppermute(value, axis, [(source, source + steps) for source in range(leading, last)])


def swap(value, axis, bit):
    count = lax.axis_size(axis)
    return lax.ppermute(value, axis, [(i, i ^ (1 << bit)) for i in range(count)])


def bit_count(axis):
    count = lax.axis_size(axis)
    bits = count.bit_length() - 1
    assert count == 1 << bits
    return bits


def scatter_sum(value, axis):
    index = lax.axis_index(axis)
    for bit in range(bit_count(axis)):
        value = value.reshape((value.shape[0] // 2, 2) + value.shape[1:])
        mine = (index >> bit) & 1
        kept = lax.dynamic_index_in_dim(value, mine, 1, keepdims=False)
        sent = lax.dynamic_index_in_dim(value, 1 - mine, 1, keepdims=False)
        value = (kept.astype(F32) + swap(sent, axis, bit).astype(F32)).astype(BF16)
    return value[0]


def gather_all(value, axis):
    index = lax.axis_index(axis)
    value = value[None]
    for bit in reversed(range(bit_count(axis))):
        other = swap(value, axis, bit)
        low_bit = ((index >> bit) & 1) == 0
        first = jnp.where(low_bit, value, other)
        second = jnp.where(low_bit, other, value)
        value = jnp.stack([first, second], axis=1)
        value = value.reshape((2 * value.shape[0],) + value.shape[2:])
    return value


def after(values, event):
    return lax.optimization_barrier((values, event))[0]


def gather_rows(value, axis):
    index = lax.axis_index(axis)
    count = lax.axis_size(axis)
    rows = value.shape[0]
    pieces = [(0, value)]
    for bit in reversed(range(bit_count(axis))):
        pieces += [(away | (1 << bit), swap(piece, axis, bit)) for away, piece in pieces]
    whole = jnp.zeros((count * rows, value.shape[1]), value.dtype)
    for away, piece in pieces:
        whole = lax.dynamic_update_slice(whole, piece, ((index ^ away) * rows, 0))
    return whole


def reduce_ctx(owned):
    flat = jnp.concatenate([part.reshape(-1) for part in owned])
    count = lax.axis_size("ctx")
    unit = count * 16 * 128
    size = flat.shape[0]
    padded = -(-size // unit) * unit
    if padded != size:
        flat = jnp.pad(flat, (0, padded - size))
    part = scatter_sum(flat.reshape(count, -1, 128), "ctx")
    return gather_all(part, "ctx").reshape(-1)[:size].astype(F32)


def rms_scale(value_tensor, gain_vec):
    return (
        value_tensor
        * lax.rsqrt(jnp.mean(value_tensor * value_tensor, axis=-1, keepdims=True) + EPSILON)
        * gain_vec
    )


def rotary_tables(token_positions):
    half_dim = HEAD_SIZE // 2
    spacing = jnp.arange(half_dim, dtype=F32) * (2.0 / HEAD_SIZE)
    frequency = F32(ROPE_BASE) ** (-spacing)
    angles = frequency[:, None] * token_positions.astype(F32)[None, :]
    return jnp.cos(angles), jnp.sin(angles)


def rotate(value, cosine, sine):
    rows = value.shape[1]
    halves = value.reshape(-1, 2, HEAD_SIZE // 2, rows)
    first, second = halves[:, 0], halves[:, 1]
    turned = jnp.stack(
        [first * cosine - second * sine, second * cosine + first * sine], axis=1
    )
    return turned.reshape(value.shape)


def row_limits(row_ids, lengths, group_rows):
    padded = (lengths + BLK - 1) // BLK * BLK
    rel_ends = jnp.cumsum(padded)
    offset = group_rows - BLK - rel_ends[-1]
    seq_ends = rel_ends + offset
    starts = seq_ends - padded
    used_end = seq_ends[-1]
    inside = (row_ids[:, None] >= starts[None, :]) & (row_ids[:, None] < seq_ends[None, :])
    anywhere = jnp.any(inside, axis=1)
    outside_first = jnp.where(row_ids < offset, 0, used_end)
    first_row = jnp.where(
        anywhere, jnp.sum(jnp.where(inside, starts[None, :], 0), axis=1), outside_first
    )
    valid_end = jnp.sum(jnp.where(inside, (starts + lengths)[None, :], 0), axis=1)
    key_from = jnp.where(anywhere, first_row, row_ids)
    key_to = jnp.where(anywhere, jnp.minimum(row_ids + 1, valid_end), row_ids)
    return row_ids - first_row, key_from, key_to


def contract(left, right, left_dim, right_dim):
    return lax.dot_general(
        left, right, (((left_dim,), (right_dim,)), ((), ())), preferred_element_type=F32
    )


def allowed_keys(limits_ref, chunk_start, rows):
    key_ids = lax.broadcasted_iota(jnp.int32, (CHUNK, rows), 0) + chunk_start
    return ((key_ids >= limits_ref[0:1, :]) & (key_ids < limits_ref[1:2, :])) | (
        key_ids == limits_ref[2:3, :]
    )


def attend_kernel(first_ref, query_ref, kv_ref, limits_ref, out_ref, sums_ref, total_ref):
    rows = query_ref.shape[1]
    chunks = kv_ref.shape[2] // CHUNK
    total_ref[...] = jnp.zeros_like(total_ref)

    def step(chunk, carry):
        start = pl.multiple_of(chunk * CHUNK, CHUNK)
        keys = kv_ref[0, :, pl.ds(start, CHUNK)]
        values = kv_ref[1, :, pl.ds(start, CHUNK)]
        allowed = allowed_keys(limits_ref, start, rows)
        carry = list(carry)
        for head in range(HEADS_PER_GROUP):
            cut = slice(head * HEAD_SIZE, (head + 1) * HEAD_SIZE)
            peak, summed = carry[2 * head], carry[2 * head + 1]
            scores = contract(keys, query_ref[cut, :], 0, 0)
            scores = jnp.where(allowed, scores, LOWEST)
            new_peak = jnp.maximum(peak, jnp.max(scores, axis=0, keepdims=True))
            raised = jnp.exp(scores - new_peak)
            fade = jnp.exp(peak - new_peak)
            carry[2 * head] = new_peak
            carry[2 * head + 1] = summed * fade + jnp.sum(raised, axis=0, keepdims=True)
            total_ref[cut, :] = total_ref[cut, :] * fade + contract(
                values, raised.astype(BF16), 1, 0
            )
        return tuple(carry)

    start_carry = (
        jnp.full((1, rows), LOWEST, F32),
        jnp.zeros((1, rows), F32),
    ) * HEADS_PER_GROUP
    carry = lax.fori_loop(first_ref[0], chunks, step, start_carry)
    for head in range(HEADS_PER_GROUP):
        cut = slice(head * HEAD_SIZE, (head + 1) * HEAD_SIZE)
        peak, summed = carry[2 * head], carry[2 * head + 1]
        out_ref[cut, :] = (total_ref[cut, :] / summed).astype(BF16)
        sums_ref[0, head : head + 1, :] = peak + jnp.log(summed)


def attend_back_kernel(
    first_ref,
    query_ref,
    grad_ref,
    kv_ref,
    limits_ref,
    sums_ref,
    delta_ref,
    grad_query_ref,
    grad_kv_ref,
):
    rows = query_ref.shape[1]
    chunks = kv_ref.shape[2] // CHUNK
    first = first_ref[0]
    grad_query_ref[...] = jnp.zeros_like(grad_query_ref)

    def clear(chunk, carry):
        start = pl.multiple_of(chunk * CHUNK, CHUNK)
        grad_kv_ref[:, :, pl.ds(start, CHUNK)] = jnp.zeros((2, HEAD_SIZE, CHUNK), BF16)
        return carry

    lax.fori_loop(0, first, clear, 0)

    def step(chunk, carry):
        start = pl.multiple_of(chunk * CHUNK, CHUNK)
        keys = kv_ref[0, :, pl.ds(start, CHUNK)]
        values = kv_ref[1, :, pl.ds(start, CHUNK)]
        allowed = allowed_keys(limits_ref, start, rows)
        grad_keys = jnp.zeros((HEAD_SIZE, CHUNK), F32)
        grad_values = jnp.zeros((HEAD_SIZE, CHUNK), F32)
        for head in range(HEADS_PER_GROUP):
            cut = slice(head * HEAD_SIZE, (head + 1) * HEAD_SIZE)
            query = query_ref[cut, :]
            grad = grad_ref[cut, :]
            scores = contract(keys, query, 0, 0)
            scores = jnp.where(allowed, scores, LOWEST)
            softmax = jnp.exp(scores - sums_ref[0, head : head + 1, :])
            grad_probs = contract(values, grad, 0, 0)
            grad_scores = softmax * (grad_probs - delta_ref[0, head : head + 1, :])
            low_scores = grad_scores.astype(BF16)
            grad_values += contract(grad, softmax.astype(BF16), 1, 1)
            grad_keys += contract(query, low_scores, 1, 1)
            grad_query_ref[cut, :] += contract(keys, low_scores, 1, 0)
        grad_kv_ref[0, :, pl.ds(start, CHUNK)] = grad_keys.astype(BF16)
        grad_kv_ref[1, :, pl.ds(start, CHUNK)] = grad_values.astype(BF16)
        return carry

    lax.fori_loop(first, chunks, step, 0)


def group_block(rows):
    return pl.BlockSpec((GROUP_WIDTH, rows), lambda group, first: (group, 0))


def window_block(window):
    return pl.BlockSpec((2, HEAD_SIZE, window), lambda group, first: (0, group, 0))


def stat_block(rows):
    return pl.BlockSpec((1, HEADS_PER_GROUP, rows), lambda group, first: (group, 0, 0))


def limits_block(rows):
    return pl.BlockSpec((3, rows), lambda group, first: (0, 0))


def attend(first, queries, window_kv, limits):
    rows, window = queries.shape[1], window_kv.shape[2]
    return pl.pallas_call(
        attend_kernel,
        grid_spec=pltpu.PrefetchScalarGridSpec(
            num_scalar_prefetch=1,
            grid=(KEY_VALUE_HEADS,),
            in_specs=[group_block(rows), window_block(window), limits_block(rows)],
            out_specs=[group_block(rows), stat_block(rows)],
            scratch_shapes=[pltpu.VMEM((GROUP_WIDTH, rows), F32)],
        ),
        out_shape=[
            jax.ShapeDtypeStruct((QUERY_WIDTH, rows), BF16),
            jax.ShapeDtypeStruct((KEY_VALUE_HEADS, HEADS_PER_GROUP, rows), F32),
        ],
        cost_estimate=pl.CostEstimate(
            flops=60 * QUERY_WIDTH * rows * window,
            bytes_accessed=4 * KV_WIDTH * window,
            transcendentals=QUERY_HEADS * rows * window,
        ),
        compiler_params=pltpu.CompilerParams(vmem_limit_bytes=32 << 20),
    )(first, queries, window_kv, limits)


def attend_back(first, queries, grads, window_kv, limits, sums, delta):
    rows, window = queries.shape[1], window_kv.shape[2]
    return pl.pallas_call(
        attend_back_kernel,
        grid_spec=pltpu.PrefetchScalarGridSpec(
            num_scalar_prefetch=1,
            grid=(KEY_VALUE_HEADS,),
            in_specs=[
                group_block(rows),
                group_block(rows),
                window_block(window),
                limits_block(rows),
                stat_block(rows),
                stat_block(rows),
            ],
            out_specs=[group_block(rows), window_block(window)],
        ),
        out_shape=[
            jax.ShapeDtypeStruct((QUERY_WIDTH, rows), F32),
            jax.ShapeDtypeStruct((2, KV_WIDTH, window), BF16),
        ],
        cost_estimate=pl.CostEstimate(
            flops=120 * QUERY_WIDTH * rows * window,
            bytes_accessed=8 * KV_WIDTH * window,
            transcendentals=QUERY_HEADS * rows * window,
        ),
        compiler_params=pltpu.CompilerParams(vmem_limit_bytes=32 << 20),
    )(first, queries, grads, window_kv, limits, sums, delta)


def collect_window(own_pair, reach_back):
    pieces = [from_behind(own_pair, "ctx", distance) for distance in range(reach_back, 0, -1)]
    window = jnp.concatenate(pieces + [own_pair], axis=1)
    return window.reshape(2, KV_WIDTH, -1)


def return_grads(window_grad, reach_back, rows):
    totals = window_grad[:, reach_back * rows :].astype(F32)
    for distance in range(1, reach_back + 1):
        piece = window_grad[:, (reach_back - distance) * rows : (reach_back - distance + 1) * rows]
        totals = totals + from_behind(piece, "ctx", -distance).astype(F32)
    return totals


def layer_forward(residual, weights, tables, first, limits, reach_back):
    qkv_mat, out_mat, gate_up_mat, down_mat, attn_scale, ffn_scale = weights
    cosine, sine = tables
    normed_a = rms_scale(residual, attn_scale).astype(BF16)
    projected = contract(qkv_mat, normed_a, 0, 1)
    rotated = rotate(projected[: QUERY_WIDTH + KV_WIDTH], cosine, sine)
    queries = rotated[:QUERY_WIDTH].astype(BF16) * BF16(HEAD_SIZE ** (-0.5))
    own_pair = jnp.concatenate(
        [rotated[QUERY_WIDTH:].astype(BF16), projected[QUERY_WIDTH + KV_WIDTH :].astype(BF16)],
        axis=0,
    )
    window_kv = collect_window(own_pair, reach_back)
    attended, sums = attend(first, queries, window_kv, limits)
    residual_mid = residual + contract(attended, out_mat, 0, 0)
    normed_f = rms_scale(residual_mid, ffn_scale).astype(BF16)
    gate_up = contract(normed_f, gate_up_mat, 1, 0)
    half = gate_up.shape[1] // 2
    gate_act, up_act = gate_up[:, :half], gate_up[:, half:]
    hidden = (jax.nn.silu(gate_act) * up_act).astype(BF16)
    residual_out = residual_mid + contract(hidden, down_mat, 1, 0)
    record = (
        residual,
        normed_a,
        queries,
        window_kv,
        attended,
        sums,
        residual_mid,
        normed_f,
        gate_act,
        up_act,
        hidden,
    )
    return residual_out, record


def layer_backward(grad_res, weights, record, tables, first, limits, reach_back, later_owned):
    qkv_mat, out_mat, gate_up_mat, down_mat, attn_scale, ffn_scale = weights
    cosine, sine = tables
    (
        residual,
        normed_a,
        queries,
        window_kv,
        attended,
        sums,
        residual_mid,
        normed_f,
        gate_act,
        up_act,
        hidden,
    ) = record
    rows = residual.shape[0]
    shards = lax.axis_size("shard")
    branch_f = grad_res.astype(BF16)
    grad_down_mat = contract(hidden, branch_f, 0, 0).astype(BF16)
    grad_hidden = contract(branch_f, down_mat, 1, 1)
    sigmoid_g = jax.nn.sigmoid(gate_act)
    grad_gate_up = jnp.concatenate(
        [
            (grad_hidden * up_act * sigmoid_g * (1.0 + gate_act * (1.0 - sigmoid_g))).astype(BF16),
            (grad_hidden * gate_act * sigmoid_g).astype(BF16),
        ],
        axis=1,
    )
    grad_gate_up_mat = contract(normed_f, grad_gate_up, 0, 0).astype(BF16)
    owned_gate_up = scatter_sum(
        grad_gate_up_mat.reshape(shards, -1, grad_gate_up.shape[1]), "shard"
    )
    grad_normed_f = contract(grad_gate_up, gate_up_mat, 1, 1)
    _, norm_back = jax.vjp(rms_scale, residual_mid, ffn_scale)
    grad_mid_part, grad_ffn_scale = norm_back(grad_normed_f)
    grad_mid = grad_res + grad_mid_part
    branch_a = grad_mid.astype(BF16)
    grad_out_mat = contract(attended, branch_a, 1, 0).astype(BF16)
    width = branch_a.shape[1]
    owned_down = scatter_sum(grad_down_mat.reshape(shards, -1, width), "shard")
    owned_out = scatter_sum(grad_out_mat.reshape(shards, -1, width), "shard")
    grad_attended = contract(out_mat, branch_a, 1, 1).astype(BF16)
    later_reduced = [reduce_ctx(pack) for pack in later_owned[:2]]
    if later_owned:
        grad_attended = after(grad_attended, later_owned)
    delta = jnp.sum(
        (grad_attended.astype(F32) * attended.astype(F32)).reshape(
            KEY_VALUE_HEADS, HEADS_PER_GROUP, HEAD_SIZE, rows
        ),
        axis=2,
    )
    grad_queries, window_grad = attend_back(
        first, queries, grad_attended, window_kv, limits, sums, delta
    )
    local_grad = return_grads(window_grad.reshape(2 * KV_WIDTH, -1), reach_back, rows)
    owned_gate_up, owned_down, owned_out, local_grad = lax.optimization_barrier(
        (owned_gate_up, owned_down, owned_out, local_grad)
    )
    if later_reduced:
        local_grad = after(local_grad, later_reduced)
    grad_queries = rotate(grad_queries * HEAD_SIZE ** (-0.5), cosine, -sine).astype(BF16)
    grad_keys = rotate(local_grad[:KV_WIDTH], cosine, -sine).astype(BF16)
    grad_qkv = jnp.concatenate(
        [grad_queries, grad_keys, local_grad[KV_WIDTH:].astype(BF16)], axis=0
    )
    grad_qkv_mat = contract(normed_a, grad_qkv, 0, 1).astype(BF16)
    grad_normed_a = contract(grad_qkv, qkv_mat, 0, 1)
    _, norm_back = jax.vjp(rms_scale, residual, attn_scale)
    grad_in_part, grad_attn_scale = norm_back(grad_normed_a)
    owned_qkv = scatter_sum(grad_qkv_mat.reshape(shards, -1, grad_qkv.shape[0]), "shard")
    scales = jnp.concatenate(
        [
            grad_attn_scale.astype(BF16).reshape(shards, -1),
            grad_ffn_scale.astype(BF16).reshape(shards, -1),
        ],
        axis=1,
    )
    owned = [
        [owned_gate_up],
        [owned_down, owned_out],
        [owned_qkv, scatter_sum(scales, "shard")],
    ]
    return grad_mid + grad_in_part, owned, later_reduced


def split_gradients(reduced, shards, width, hidden_width):
    reduced_gate_up, reduced_down_out, reduced_qkv = reduced
    owned = width // shards
    down_size = hidden_width // shards * width
    gate_up = reduced_gate_up.reshape(owned, 2 * hidden_width)
    qkv_size = owned * (QUERY_WIDTH + 2 * KV_WIDTH)
    qkv = reduced_qkv[:qkv_size].reshape(owned, -1)
    return (
        qkv[:, :QUERY_WIDTH],
        qkv[:, QUERY_WIDTH : QUERY_WIDTH + KV_WIDTH],
        qkv[:, QUERY_WIDTH + KV_WIDTH :],
        reduced_down_out[down_size:].reshape(owned, width),
        gate_up[:, :hidden_width],
        gate_up[:, hidden_width:],
        reduced_down_out[:down_size].reshape(-1, width),
        reduced_qkv[qkv_size : qkv_size + owned],
        reduced_qkv[qkv_size + owned :],
    )


def body(
    tokens,
    cotangent,
    seq_lengths,
    w_query,
    key_weight,
    value_weight,
    w_out,
    w_gate,
    w_up,
    w_down,
    attn_gain,
    ffn_gain,
):
    rows = tokens.shape[0]
    group_rows = rows * lax.axis_size("ctx")
    longest = min(SEQ_MOST, group_rows // 2)
    reach_back = (longest - 1) // rows + 1
    base = (lax.axis_index("ctx") - reach_back) * rows
    own_ids = lax.axis_index("ctx") * rows + jnp.arange(rows, dtype=jnp.int32)
    token_positions, key_from, key_to = row_limits(own_ids, seq_lengths[0], group_rows)
    limits = jnp.stack([key_from, key_to, own_ids], axis=0) - base
    first = jnp.clip(jnp.min(limits[0]) // CHUNK, 0, reach_back * rows // CHUNK)[None]
    tables = rotary_tables(token_positions)

    gains = gather_all(jnp.concatenate([attn_gain, ffn_gain], axis=0), "shard")
    gains = jnp.transpose(gains, (1, 0, 2)).reshape(2 * DECODER_LAYERS, -1).astype(F32)
    layer_weights = []
    event = gains
    for layer_no in range(DECODER_LAYERS):
        own_qkv = jnp.concatenate(
            [w_query[layer_no], key_weight[layer_no], value_weight[layer_no]], axis=1
        )
        if layer_no:
            own_qkv = after(own_qkv, event)
        qkv_mat = gather_rows(own_qkv, "shard")
        own_out, own_gate, own_up, own_down = after(
            (w_out[layer_no], w_gate[layer_no], w_up[layer_no], w_down[layer_no]), qkv_mat
        )
        out_mat = gather_rows(own_out, "shard")
        gate_up_mat = gather_rows(jnp.concatenate([own_gate, own_up], axis=1), "shard")
        down_mat = gather_rows(own_down, "shard")
        event = (gate_up_mat, down_mat)
        layer_weights.append(
            (qkv_mat, out_mat, gate_up_mat, down_mat)
            + (gains[layer_no], gains[DECODER_LAYERS + layer_no])
        )

    residual = tokens.astype(F32)
    records = []
    for layer_no in range(DECODER_LAYERS):
        residual, record = layer_forward(
            residual, layer_weights[layer_no], tables, first, limits, reach_back
        )
        records.append(record)
    output = residual.astype(BF16)
    grad_res = cotangent.astype(F32)
    reduced_layers = [None] * DECODER_LAYERS
    owned, qkv_packs = [], []
    for layer_no in range(DECODER_LAYERS - 1, -1, -1):
        grad_res, owned, later_reduced = layer_backward(
            grad_res,
            layer_weights[layer_no],
            records[layer_no],
            tables,
            first,
            limits,
            reach_back,
            owned,
        )
        qkv_packs += owned[2]
        if layer_no < DECODER_LAYERS - 1:
            reduced_layers[layer_no + 1] = later_reduced
    reduced_layers[0] = [reduce_ctx(pack) for pack in owned[:2]]
    both_qkv = jnp.split(reduce_ctx(qkv_packs), DECODER_LAYERS)
    reduced_layers = [
        reduced + [qkv] for reduced, qkv in zip(reduced_layers, reversed(both_qkv))
    ]
    shards, width, hidden_width = lax.axis_size("shard"), tokens.shape[1], w_gate.shape[2]
    reduced_layers = [
        split_gradients(reduced, shards, width, hidden_width) for reduced in reduced_layers
    ]
    token_grad = grad_res.astype(BF16)
    stacked = tuple(
        jnp.stack([reduced_layers[layer_no][member] for layer_no in range(DECODER_LAYERS)], axis=0)
        for member in range(9)
    )
    return (output, token_grad) + stacked


def solution(mesh):
    placed = (
        P(("shard", "ctx"), None),
        P(("shard", "ctx"), None),
        P("shard", None),
        P(None, "shard", None),
        P(None, "shard", None),
        P(None, "shard", None),
        P(None, "shard", None),
        P(None, "shard", None),
        P(None, "shard", None),
        P(None, "shard", None),
        P(None, "shard"),
        P(None, "shard"),
    )
    return jax.shard_map(
        body,
        mesh=mesh,
        in_specs=placed,
        out_specs=(
            P(("shard", "ctx"), None),
            P(("shard", "ctx"), None),
            P(None, "shard", None),
            P(None, "shard", None),
            P(None, "shard", None),
            P(None, "shard", None),
            P(None, "shard", None),
            P(None, "shard", None),
            P(None, "shard", None),
            P(None, "shard"),
            P(None, "shard"),
        ),
        check_vma=False,
    )
```
